32 devices in a mesh: virt: 8 (over z, x), pair: 4 (over y, core).
Axes of the slice: x: 2, y: 2, z: 4, core: 2. Of those that a mesh axis runs over, the one named last changes fastest.
Arguments:
- amplitudes: bfloat16 [8, 1024, 2, 1024], P('pair'), may hold values from -6 to 6
- integrals: bfloat16 [2, 512, 8, 65536], P(None, None, None, ('virt', 'pair')), may hold values from -0.125 to 0.125
- virt_counts: int32 [8], replicated, may hold values from 32 to 64, as said below
- pair_counts: int32 [8], replicated, may hold values from 512 to 1024, as said below
- pair_list: int32 [8, 1024, 2], P('pair'), may hold values from 0 to 99
- eps_occ: float32 [100], replicated, may hold values from -2 to -0.3
- eps_virt: float32 [512], replicated, may hold values from 0.3 to 4
Outputs:
- update: bfloat16 [8, 1024, 32768], P('pair', None, 'virt')
- pair_energy: float32 [8, 1024], P('pair', 'virt')
The draws below stay inside these ranges and needn't reach their ends.
Inputs may be any that keep to these rules, and one draw needn't show every extreme that they name: virt_counts[0] = 64; every count is at least 32. `pair_counts`: some pair symmetry has exactly 1024 pairs; every count is at least 512.
All inputs are finite; a program needn't handle non-finite values.
Results may differ from the reference program's by a relative error of at most 0.001.
Values may be sent and summed in bfloat16 or wider, within the bound.
A program may use at most 192 MiB of HBM per device.

```python
import math
import jax
import jax.numpy as jnp
from jax import lax

IRREPS = 8
NV = 512
NOCC = 100
BLK = 64
CS = 16
SLABS = 2
KS = 1024
PCAP = 1024


def draw_virt_counts(key, part):
    counts = jax.random.randint(key, (IRREPS,), BLK // 2, BLK + 1)
    return counts.at[0].set(BLK).astype(jnp.int32)


def draw_pair_counts(key, part):
    first, second = jax.random.split(jax.random.fold_in(key, 11))
    counts = jax.random.randint(first, (IRREPS,), PCAP // 2, PCAP + 1)
    where_full = jax.random.randint(second, (), 0, IRREPS)
    return counts.at[where_full].set(PCAP).astype(jnp.int32)


def set_ends(entries, stream_key, smallest, largest):
    dims = entries.shape
    index_at = [jax.random.randint(jax.random.fold_in(stream_key, axis), (), 0, dims[axis]) for axis in range(len(dims))]
    entries = entries.at[tuple(index_at)].set(smallest)
    longest = dims.index(max(dims))
    index_at[longest] = (index_at[longest] + 1) % dims[longest]
    return entries.at[tuple(index_at)].set(largest)


def levels(stream_key, dims, cuts, least, largest):
    factor_of = 1.0
    for position, shards_of in cuts:
        heights = jax.random.uniform(jax.random.fold_in(jax.random.fold_in(stream_key, 6), position), (shards_of,), jnp.float32, least / len(cuts), largest / len(cuts))
        factor_of = factor_of * jnp.repeat(jnp.exp(heights), dims[position] // shards_of).reshape((-1,) + (1,) * (len(dims) - 1 - position))
    return factor_of


def centred(rng, extent, deviation, limit, pieces=(), held_as=jnp.bfloat16):
    result = jax.random.normal(rng, extent, jnp.float32) * deviation
    if len(pieces) > 0:
        result = levels(rng, extent, pieces, -0.22, 0.18) * result
    return jnp.clip(result, min=-limit, max=limit).astype(held_as)


def setup_inputs(seed: int = 0) -> dict:
    seeds = jax.random.split(jax.random.key(seed), 8)
    return {
        "amplitudes": centred(seeds[0], (IRREPS, PCAP, SLABS, KS), 1.0, 6.0, ((0, 4),)),
        "integrals": centred(seeds[1], (SLABS, NV, IRREPS, BLK * KS), (KS * SLABS) ** -0.5, 0.125, ((3, 32),)),
        "virt_counts": draw_virt_counts(jax.random.fold_in(seeds[7], 71), 0),
        "pair_counts": draw_pair_counts(jax.random.fold_in(seeds[7], 71), 0),
        "pair_list": set_ends(jax.random.randint(seeds[4], (IRREPS, PCAP, 2), 0, NOCC), jax.random.fold_in(seeds[4], 1), 0, NOCC - 1).astype(jnp.int32),
        "eps_occ": jnp.clip(jax.random.uniform(seeds[5], (NOCC,), jnp.float32, -2.0, -0.3), -2.0, -0.3),
        "eps_virt": jnp.clip(jnp.exp(jax.random.uniform(seeds[6], (NV,), jnp.float32, math.log(0.3), math.log(4.0))), 0.3, 4.0),
    }


def reference(amplitudes, integrals, virt_counts, pair_counts, pair_list, eps_occ, eps_virt):
    slots = jnp.arange(BLK, dtype=jnp.int32)
    live_virt = slots[None, :] < virt_counts[:, None]
    a_index = jnp.arange(NV, dtype=jnp.int32)
    a_irrep = a_index // BLK
    a_slot = a_index % BLK
    live_a = jnp.take(live_virt.reshape(-1), a_irrep * BLK + a_slot)
    eps_table = eps_virt.reshape(IRREPS, BLK)
    row_index = jnp.arange(PCAP, dtype=jnp.int32)

    def one_irrep(h):
        dmask = jnp.tile(live_virt[h], CS).astype(jnp.bfloat16)
        masked = amplitudes[h] * dmask[None, None, :]
        ladder = jnp.zeros((PCAP, NV * BLK), jnp.float32)
        for s in range(SLABS):
            block = integrals[s][:, h, :].reshape(NV * BLK, KS)
            ladder = ladder + lax.dot_general(masked[:, s, :], block, (((1,), (1,)), ((), ())), preferred_element_type=jnp.float32)
        ladder = ladder.reshape(PCAP, NV, BLK)
        b_irrep = jnp.bitwise_xor(a_irrep, h)
        eps_b = eps_table[b_irrep]
        live_b = live_virt[b_irrep]
        pairs = pair_list[h]
        occ = eps_occ[pairs[:, 0]] + eps_occ[pairs[:, 1]]
        denom = (eps_virt[:, None] + eps_b)[None, :, :] - occ[:, None, None]
        live = (row_index < pair_counts[h])[:, None, None] & live_a[None, :, None] & live_b[None, :, :]
        ratio = jnp.where(live, ladder / denom, jnp.zeros_like(ladder))
        update = ratio.astype(jnp.bfloat16).reshape(PCAP, NV * BLK)
        energy = jnp.sum(ratio * ladder, axis=(1, 2)) / (NV * BLK)
        return update, energy

    updates, energies = lax.map(one_irrep, jnp.arange(IRREPS, dtype=jnp.int32))
    return updates, energies
```

```python
import functools

import jax
import jax.numpy as jnp
from jax import lax
from jax.experimental import pallas as pl
from jax.experimental.pallas import tpu as pltpu
from jax.sharding import PartitionSpec as P

IRREPS = 8
NV = 512
BLK = 64
CS = 16
SLABS = 2
MESH = pl.DeviceIdType.MESH


def pick_counts(irrep_ids, table):
    onehot = irrep_ids[..., None] == jnp.arange(table.shape[0], dtype=jnp.int32)
    return jnp.sum(jnp.where(onehot, table, 0), axis=-1)


def shards(amplitudes, integrals, virt_counts, pair_counts, pair_list, eps_occ, eps_virt):
    local_irreps = amplitudes.shape[0]
    rows = amplitudes.shape[1]
    width = amplitudes.shape[3]
    n_virt = lax.axis_size("virt")
    n_pair = lax.axis_size("pair")
    a_local = NV // n_virt
    irrep_ids = lax.axis_index("pair") * local_irreps + jnp.arange(local_irreps, dtype=jnp.int32)
    slots = jnp.arange(BLK, dtype=jnp.int32)
    live_d = slots[None, :] < pick_counts(irrep_ids, virt_counts)[:, None]
    dmask = jnp.tile(live_d, (1, CS)).astype(jnp.bfloat16)
    masked = amplitudes * dmask[:, None, None, :]
    ladder = jnp.zeros((local_irreps, rows, a_local, BLK), jnp.float32)
    for s in range(SLABS):
        piece = integrals[s]
        moved = lax.all_to_all(
            lax.all_to_all(piece, "virt", split_axis=0, concat_axis=2, tiled=True),
            "pair",
            split_axis=1,
            concat_axis=2,
            tiled=True,
        )
        moved = moved.reshape(a_local, local_irreps, n_pair, n_virt, -1)
        moved = jnp.transpose(moved, (0, 1, 3, 2, 4)).reshape(a_local, local_irreps, BLK, width)
        ladder = ladder + jnp.einsum(
            "hrk,ahsk->hras", masked[:, :, s, :], moved, preferred_element_type=jnp.float32
        )
    a_global = lax.axis_index("virt") * a_local + jnp.arange(a_local, dtype=jnp.int32)
    a_irrep = a_global // BLK
    a_slot = a_global % BLK
    live_a = a_slot < pick_counts(a_irrep, virt_counts)
    eps_a = lax.dynamic_slice_in_dim(eps_virt, lax.axis_index("virt") * a_local, a_local)
    b_irrep = jnp.bitwise_xor(a_irrep[None, :], irrep_ids[:, None])
    b_onehot = (b_irrep[..., None] == jnp.arange(IRREPS, dtype=jnp.int32)).astype(jnp.float32)
    eps_table = eps_virt.reshape(IRREPS, BLK)
    eps_b = jnp.einsum("hag,gs->has", b_onehot, eps_table, precision=lax.Precision.HIGHEST)
    live_b = slots[None, None, :] < pick_counts(b_irrep, virt_counts)[..., None]
    occ_onehot = pair_list[..., None] == jnp.arange(eps_occ.shape[0], dtype=jnp.int32)
    occ_terms = jnp.sum(jnp.where(occ_onehot, eps_occ, 0.0), axis=-1)
    occ = occ_terms[:, :, 0] + occ_terms[:, :, 1]
    live_rows = (
        jnp.arange(rows, dtype=jnp.int32)[None, :] < pick_counts(irrep_ids, pair_counts)[:, None]
    )
    denom = (eps_a[None, :, None] + eps_b)[:, None, :, :] - occ[:, :, None, None]
    live = live_rows[:, :, None, None] & live_a[None, None, :, None] & live_b[:, None, :, :]
    ratio = jnp.where(live, ladder / denom, jnp.zeros_like(ladder))
    update = ratio.astype(jnp.bfloat16).reshape(local_irreps, rows, a_local * BLK)
    partial_value = jnp.sum(ratio * ladder, axis=(2, 3)) / (NV * BLK)
    energy = lax.psum_scatter(partial_value, "virt", scatter_dimension=1, tiled=True)
    return (update, energy)


def flip_bits(index, pattern, count):
    flipped = 0
    weight = 1
    while weight < count:
        bit = (index // weight) % 2
        mine = (pattern // weight) % 2
        flipped = flipped + weight * (bit + mine - 2 * bit * mine)
        weight *= 2
    return flipped


def ladder_kernel(
    n_virt, n_pair, irreps_here, a_local, parts_sb,
    eri_ref, amps_ref, rows_ref, occ_ref, sort_in_ref, sort_out_ref,
    got_ref, recv_ref, energy_ref,
    x_buf, stage, y_buf, out_buf,
    x_sem, y_sem, own_sem, send_sem, recv_sem, out_sem, got_sem,
):
    me_v = lax.axis_index("virt")
    me_p = lax.axis_index("pair")
    slabs = eri_ref.shape[0]
    loc = eri_ref.shape[2]
    irreps = irreps_here * n_pair
    ks = amps_ref.shape[2]
    nrows = amps_ref.shape[3]
    sort_rows = sort_in_ref.shape[0]
    a_sort = sort_rows // irreps
    sb_here = n_pair * parts_sb
    chunk_rows = a_local * irreps
    tile_n = 512
    tile_r = 256

    barrier = pltpu.get_barrier_semaphore()
    for d in range(1, n_pair):
        pl.semaphore_signal(barrier, inc=1, device_id=(me_v, flip_bits(me_p, d, n_pair)), device_id_type=MESH)
    for d in range(1, n_virt):
        pl.semaphore_signal(barrier, inc=1, device_id=(flip_bits(me_v, d, n_virt), me_p), device_id_type=MESH)
    pl.semaphore_wait(barrier, n_pair - 1 + n_virt - 1)

    def target(t):
        return flip_bits(me_v, n_virt - 1 - t, n_virt)

    def pair_copy(t, d):
        peer = flip_bits(me_p, d, n_pair)
        return pltpu.make_async_remote_copy(
            src_ref=stage.at[t % 2, peer],
            dst_ref=recv_ref.at[t, me_p],
            send_sem=send_sem.at[t % 2, d - 1],
            recv_sem=recv_sem.at[t, d - 1],
            device_id=(me_v, peer),
            device_id_type=MESH,
        )

    def own_copy(t):
        return pltpu.make_async_copy(stage.at[t % 2, me_p], recv_ref.at[t, me_p], own_sem.at[t % 2])

    def out_copy(t):
        dest = target(t)
        if t == n_virt - 1:
            return pltpu.make_async_copy(out_buf.at[t], got_ref.at[:, :, me_v], own_sem.at[2])
        return pltpu.make_async_remote_copy(
            src_ref=out_buf.at[t],
            dst_ref=got_ref.at[:, :, me_v],
            send_sem=out_sem.at[t],
            recv_sem=got_sem.at[t],
            device_id=(dest, me_p),
            device_id_type=MESH,
        )

    def prepare(t):
        dest = target(t)
        load = pltpu.make_async_copy(
            eri_ref.at[:, pl.ds(pl.multiple_of(dest * chunk_rows, chunk_rows), chunk_rows), :], x_buf, x_sem
        )
        load.start()
        load.wait()

        def sort_tile(n, carry):
            cols = pl.ds(pl.multiple_of(n * tile_n, tile_n), tile_n)
            for s in range(slabs):
                for q in range(a_local // a_sort):
                    block = x_buf[s, q * sort_rows : (q + 1) * sort_rows, cols]
                    sorted_rows = jnp.dot(
                        sort_in_ref[...], block, preferred_element_type=jnp.float32
                    ).astype(jnp.bfloat16)
                    for h in range(irreps):
                        stage[
                            t % 2, h // irreps_here, h % irreps_here, s, q * a_sort : (q + 1) * a_sort, cols
                        ] = sorted_rows[h * a_sort : (h + 1) * a_sort]
            return carry

        lax.fori_loop(0, loc // tile_n, sort_tile, 0)
        for d in range(1, n_pair):
            pair_copy(t, d).start()
        own_copy(t).start()

    def compute(t):
        dest = target(t)
        load = pltpu.make_async_copy(recv_ref.at[t], y_buf, y_sem)
        load.start()
        load.wait()
        for hh in range(irreps_here):

            def tile(n, carry):
                cols = pl.ds(pl.multiple_of(n * tile_r, tile_r), tile_r)
                ladder = None
                for s in range(slabs):
                    left = jnp.concatenate(
                        [
                            y_buf[p, hh, s, :, j * ks : (j + 1) * ks]
                            for p in range(n_pair)
                            for j in range(parts_sb)
                        ],
                        axis=0,
                    )
                    term = jnp.dot(left, amps_ref[hh, s, :, cols], preferred_element_type=jnp.float32)
                    ladder = term if ladder is None else ladder + term
                base = rows_ref[dest, :, hh : hh + 1]
                live = rows_ref[dest, :, irreps_here + hh : irreps_here + hh + 1]
                occ = occ_ref[hh : hh + 1, cols]
                live_r = occ_ref[irreps_here + hh : irreps_here + hh + 1, cols]
                denom = base - occ
                ratio = jnp.where(live * live_r > 0.5, ladder / denom, 0.0)
                energy_ref[hh : hh + 1, cols] += jnp.sum(ratio * ladder, axis=0, keepdims=True)
                update = jnp.dot(
                    sort_out_ref[...], ratio.astype(jnp.bfloat16), preferred_element_type=jnp.float32
                ).astype(jnp.bfloat16)
                out_buf[t, hh, :, :, cols] = update.reshape(a_local, sb_here, tile_r)
                return carry

            lax.fori_loop(0, nrows // tile_r, tile, 0)
        out_copy(t).start()

    energy_ref[...] = jnp.zeros_like(energy_ref)
    prepare(0)
    prepare(1)
    for t in range(n_virt):
        for d in range(1, n_pair):
            pair_copy(t, d).wait_recv()
        own_copy(t).wait()
        compute(t)
        for d in range(1, n_pair):
            pair_copy(t, d).wait_send()
        if t + 2 < n_virt:
            prepare(t + 2)
    for t in range(n_virt):
        out_copy(t).wait()


def fused_shards(amplitudes, integrals, virt_counts, pair_counts, pair_list, eps_occ, eps_virt):
    irreps_here, rows, slabs, ks = amplitudes.shape
    n_virt = lax.axis_size("virt")
    n_pair = lax.axis_size("pair")
    nv = integrals.shape[1]
    irreps = integrals.shape[2]
    loc = integrals.shape[3]
    a_local = nv // n_virt
    parts_sb = loc // ks
    sb_here = n_pair * parts_sb
    me_v = lax.axis_index("virt")
    irrep_ids = lax.axis_index("pair") * irreps_here + jnp.arange(irreps_here, dtype=jnp.int32)
    slots = jnp.arange(BLK, dtype=jnp.int32)
    live_d = slots[None, :] < pick_counts(irrep_ids, virt_counts)[:, None]
    dmask = jnp.tile(live_d, (1, ks // BLK)).astype(jnp.bfloat16)
    masked = amplitudes * dmask[:, None, None, :]
    amps = jnp.transpose(masked, (0, 2, 3, 1))

    a_index = jnp.arange(nv, dtype=jnp.int32)
    a_irrep = a_index // BLK
    live_virt = (slots[None, :] < virt_counts[:, None]).astype(jnp.float32)
    b_irrep = jnp.bitwise_xor(a_irrep[None, :], irrep_ids[:, None])
    b_onehot = (b_irrep[..., None] == jnp.arange(irreps, dtype=jnp.int32)).astype(jnp.float32)
    eps_here = lax.dynamic_slice_in_dim(eps_virt.reshape(irreps, BLK), me_v * sb_here, sb_here, axis=1)
    live_here = lax.dynamic_slice_in_dim(live_virt, me_v * sb_here, sb_here, axis=1)
    eps_b = jnp.einsum("hag,gs->hsa", b_onehot, eps_here, precision=lax.Precision.HIGHEST)
    live_b = jnp.einsum("hag,gs->hsa", b_onehot, live_here, precision=lax.Precision.HIGHEST)
    base = eps_virt[None, None, :] + eps_b
    live = live_virt.reshape(-1)[None, None, :] * live_b
    cols = jnp.concatenate([base, live], axis=0)
    cols = cols.reshape(2 * irreps_here, sb_here, n_virt, a_local)
    cols = jnp.transpose(cols, (2, 1, 3, 0)).reshape(n_virt, sb_here * a_local, 2 * irreps_here)

    occ_onehot = pair_list[..., None] == jnp.arange(eps_occ.shape[0], dtype=jnp.int32)
    occ_terms = jnp.sum(jnp.where(occ_onehot, eps_occ, 0.0), axis=-1)
    occ = occ_terms[:, :, 0] + occ_terms[:, :, 1]
    live_rows = jnp.arange(rows, dtype=jnp.int32)[None, :] < pick_counts(irrep_ids, pair_counts)[:, None]
    occ_live = jnp.concatenate([occ, live_rows.astype(jnp.float32)], axis=0)

    a_sort = 32
    n_in = a_sort * irreps
    i_in = jnp.arange(n_in, dtype=jnp.int32)
    from_in = (i_in % a_sort) * irreps + i_in // a_sort
    sort_in = (from_in[:, None] == i_in[None, :]).astype(jnp.bfloat16)
    i_out = jnp.arange(a_local * sb_here, dtype=jnp.int32)
    from_out = (i_out % sb_here) * a_local + i_out // sb_here
    sort_out = (from_out[:, None] == i_out[None, :]).astype(jnp.bfloat16)

    eri = integrals.reshape(slabs, nv * irreps, loc)
    vmem = pl.BlockSpec(memory_space=pltpu.VMEM)
    hbm = pl.BlockSpec(memory_space=pl.ANY)
    got, _, energy = pl.pallas_call(
        functools.partial(ladder_kernel, n_virt, n_pair, irreps_here, a_local, parts_sb),
        out_shape=(
            jax.ShapeDtypeStruct((irreps_here, a_local, n_virt, sb_here, rows), jnp.bfloat16),
            jax.ShapeDtypeStruct((n_virt, n_pair, irreps_here, slabs, a_local, loc), jnp.bfloat16),
            jax.ShapeDtypeStruct((irreps_here, rows), jnp.float32),
        ),
        in_specs=[hbm, vmem, vmem, vmem, vmem, vmem],
        out_specs=(hbm, hbm, vmem),
        scratch_shapes=[
            pltpu.VMEM((slabs, a_local * irreps, loc), jnp.bfloat16),
            pltpu.VMEM((2, n_pair, irreps_here, slabs, a_local, loc), jnp.bfloat16),
            pltpu.VMEM((n_pair, irreps_here, slabs, a_local, loc), jnp.bfloat16),
            pltpu.VMEM((n_virt, irreps_here, a_local, sb_here, rows), jnp.bfloat16),
            pltpu.SemaphoreType.DMA,
            pltpu.SemaphoreType.DMA,
            pltpu.SemaphoreType.DMA((3,)),
            pltpu.SemaphoreType.DMA((2, n_pair - 1)),
            pltpu.SemaphoreType.DMA((n_virt, n_pair - 1)),
            pltpu.SemaphoreType.DMA((n_virt,)),
            pltpu.SemaphoreType.DMA((n_virt,)),
        ],
        compiler_params=pltpu.CompilerParams(
            collective_id=0, has_side_effects=True, vmem_limit_bytes=60 * 1024 * 1024
        ),
    )(eri, amps, cols, occ_live, sort_in, sort_out)
    flat = got.reshape(irreps_here, a_local * BLK, rows)
    update = jnp.transpose(flat, (0, 2, 1))
    energy = lax.psum_scatter(energy / (nv * BLK), "virt", scatter_dimension=1, tiled=True)
    return (update, energy)


def solution(mesh):
    placed = (
        P("pair", None, None, None),
        P(None, None, None, ("virt", "pair")),
        P(),
        P(),
        P("pair", None, None),
        P(),
        P(),
    )

    def run(*arrays):
        amplitudes, integrals = arrays[:2]
        loc = integrals.shape[3] // (mesh.shape["virt"] * mesh.shape["pair"])
        whole_slots = loc % amplitudes.shape[3] == 0
        whole_chunks = (integrals.shape[1] // mesh.shape["virt"]) % 32 == 0
        body = fused_shards if whole_slots and whole_chunks else shards
        return jax.shard_map(
            body,
            mesh=mesh,
            in_specs=placed,
            out_specs=(P("pair", None, "virt"), P("pair", "virt")),
            check_vma=False,
        )(*arrays)

    return run
```

```python
import functools

import jax
import jax.numpy as jnp
from jax import lax
from jax.experimental import pallas as pl
from jax.experimental.pallas import tpu as pltpu
from jax.sharding import PartitionSpec as P

IRREPS = 8
NV = 512
BLK = 64
CS = 16
SLABS = 2
A_SORT = 32
MESH = pl.DeviceIdType.MESH


def pick_counts(irrep_ids, table):
    onehot = irrep_ids[..., None] == jnp.arange(table.shape[0], dtype=jnp.int32)
    return jnp.sum(jnp.where(onehot, table, 0), axis=-1)


def shards(amplitudes, integrals, virt_counts, pair_counts, pair_list, eps_occ, eps_virt):
    local_irreps = amplitudes.shape[0]
    rows = amplitudes.shape[1]
    width = amplitudes.shape[3]
    n_virt = lax.axis_size("virt")
    n_pair = lax.axis_size("pair")
    a_local = NV // n_virt
    irrep_ids = lax.axis_index("pair") * local_irreps + jnp.arange(local_irreps, dtype=jnp.int32)
    slots = jnp.arange(BLK, dtype=jnp.int32)
    live_d = slots[None, :] < pick_counts(irrep_ids, virt_counts)[:, None]
    dmask = jnp.tile(live_d, (1, CS)).astype(jnp.bfloat16)
    masked = amplitudes * dmask[:, None, None, :]
    ladder = jnp.zeros((local_irreps, rows, a_local, BLK), jnp.float32)
    for s in range(SLABS):
        piece = integrals[s]
        moved = lax.all_to_all(
            lax.all_to_all(piece, "virt", split_axis=0, concat_axis=2, tiled=True),
            "pair",
            split_axis=1,
            concat_axis=2,
            tiled=True,
        )
        moved = moved.reshape(a_local, local_irreps, n_pair, n_virt, -1)
        moved = jnp.transpose(moved, (0, 1, 3, 2, 4)).reshape(a_local, local_irreps, BLK, width)
        ladder = ladder + jnp.einsum(
            "hrk,ahsk->hras", masked[:, :, s, :], moved, preferred_element_type=jnp.float32
        )
    a_global = lax.axis_index("virt") * a_local + jnp.arange(a_local, dtype=jnp.int32)
    a_irrep = a_global // BLK
    a_slot = a_global % BLK
    live_a = a_slot < pick_counts(a_irrep, virt_counts)
    eps_a = lax.dynamic_slice_in_dim(eps_virt, lax.axis_index("virt") * a_local, a_local)
    b_irrep = jnp.bitwise_xor(a_irrep[None, :], irrep_ids[:, None])
    b_onehot = (b_irrep[..., None] == jnp.arange(IRREPS, dtype=jnp.int32)).astype(jnp.float32)
    eps_table = eps_virt.reshape(IRREPS, BLK)
    eps_b = jnp.einsum("hag,gs->has", b_onehot, eps_table, precision=lax.Precision.HIGHEST)
    live_b = slots[None, None, :] < pick_counts(b_irrep, virt_counts)[..., None]
    occ_onehot = pair_list[..., None] == jnp.arange(eps_occ.shape[0], dtype=jnp.int32)
    occ_terms = jnp.sum(jnp.where(occ_onehot, eps_occ, 0.0), axis=-1)
    occ = occ_terms[:, :, 0] + occ_terms[:, :, 1]
    live_rows = (
        jnp.arange(rows, dtype=jnp.int32)[None, :] < pick_counts(irrep_ids, pair_counts)[:, None]
    )
    denom = (eps_a[None, :, None] + eps_b)[:, None, :, :] - occ[:, :, None, None]
    live = live_rows[:, :, None, None] & live_a[None, None, :, None] & live_b[:, None, :, :]
    ratio = jnp.where(live, ladder / denom, jnp.zeros_like(ladder))
    update = ratio.astype(jnp.bfloat16).reshape(local_irreps, rows, a_local * BLK)
    partial_value = jnp.sum(ratio * ladder, axis=(2, 3)) / (NV * BLK)
    energy = lax.psum_scatter(partial_value, "virt", scatter_dimension=1, tiled=True)
    return (update, energy)


def flip_bits(index, pattern, count):
    flipped = 0
    weight = 1
    while weight < count:
        bit = (index // weight) % 2
        mine = (pattern // weight) % 2
        flipped = flipped + weight * (bit + mine - 2 * bit * mine)
        weight *= 2
    return flipped


def ladder_kernel(
    n_virt, n_pair, irreps_here, a_chunk, cuts, depth, parts_sb, energy_scale,
    eri_ref, amps_ref, rows_ref, occ_ref, sort_in_ref, sort_out_ref,
    got_ref, recv_ref, energy_ref,
    x_buf, stage, y_buf, out_buf, terms, parts,
    x_sem, y_sem, own_sem, keep_sem, send_sem, recv_sem, out_sem, got_sem, term_sem, part_sem,
):
    me_v = lax.axis_index("virt")
    me_p = lax.axis_index("pair")
    slabs = eri_ref.shape[0]
    loc = eri_ref.shape[2]
    irreps = irreps_here * n_pair
    ks = amps_ref.shape[2]
    nrows = amps_ref.shape[3]
    sort_rows = sort_in_ref.shape[0]
    a_sort = sort_rows // irreps
    sb_here = n_pair * parts_sb
    chunk_rows = a_chunk * irreps
    steps = n_virt * cuts
    e_cols = nrows // n_virt
    tile_n = 512
    tile_r = 256

    barrier = pltpu.get_barrier_semaphore()
    for d in range(1, n_pair):
        pl.semaphore_signal(barrier, inc=1, device_id=(me_v, flip_bits(me_p, d, n_pair)), device_id_type=MESH)
    for d in range(1, n_virt):
        pl.semaphore_signal(barrier, inc=1, device_id=(flip_bits(me_v, d, n_virt), me_p), device_id_type=MESH)
    pl.semaphore_wait(barrier, n_pair - 1 + n_virt - 1)

    def target(t):
        return flip_bits(me_v, n_virt - 1 - t // cuts, n_virt)

    def pair_copy(t, d):
        peer = flip_bits(me_p, d, n_pair)
        return pltpu.make_async_remote_copy(
            src_ref=stage.at[t % depth, peer],
            dst_ref=recv_ref.at[t, me_p],
            send_sem=send_sem.at[t % depth, d - 1],
            recv_sem=recv_sem.at[t, d - 1],
            device_id=(me_v, peer),
            device_id_type=MESH,
        )

    def own_copy(t):
        return pltpu.make_async_copy(stage.at[t % depth, me_p], recv_ref.at[t, me_p], own_sem.at[t % depth])

    def out_copy(t):
        dest = target(t)
        cut = t % cuts
        there = got_ref.at[:, cut * a_chunk : (cut + 1) * a_chunk, me_v]
        if t // cuts == n_virt - 1:
            return pltpu.make_async_copy(out_buf.at[t], there, keep_sem.at[cut])
        return pltpu.make_async_remote_copy(
            src_ref=out_buf.at[t],
            dst_ref=there,
            send_sem=out_sem.at[t],
            recv_sem=got_sem.at[t],
            device_id=(dest, me_p),
            device_id_type=MESH,
        )

    def part_copy(d):
        dest = flip_bits(me_v, d, n_virt)
        cols = pl.ds(pl.multiple_of(dest * e_cols, e_cols), e_cols)
        return pltpu.make_async_remote_copy(
            src_ref=terms.at[:, cols],
            dst_ref=parts.at[d - 1],
            send_sem=term_sem.at[d - 1],
            recv_sem=part_sem.at[d - 1],
            device_id=(dest, me_p),
            device_id_type=MESH,
        )

    def prepare(t):
        dest = target(t)
        load = pltpu.make_async_copy(
            eri_ref.at[:, pl.ds(pl.multiple_of((dest * cuts + t % cuts) * chunk_rows, chunk_rows), chunk_rows), :], x_buf, x_sem
        )
        load.start()
        load.wait()

        def sort_tile(n, carry):
            cols = pl.ds(pl.multiple_of(n * tile_n, tile_n), tile_n)
            for s in range(slabs):
                for q in range(a_chunk // a_sort):
                    block = x_buf[s, q * sort_rows : (q + 1) * sort_rows, cols]
                    sorted_rows = jnp.dot(
                        sort_in_ref[...], block, preferred_element_type=jnp.float32
                    ).astype(jnp.bfloat16)
                    for h in range(irreps):
                        stage[
                            t % depth, h // irreps_here, h % irreps_here, s, q * a_sort : (q + 1) * a_sort, cols
                        ] = sorted_rows[h * a_sort : (h + 1) * a_sort]
            return carry

        lax.fori_loop(0, loc // tile_n, sort_tile, 0)
        for d in range(1, n_pair):
            pair_copy(t, d).start()
        own_copy(t).start()

    def compute(t):
        dest = target(t)
        load = pltpu.make_async_copy(recv_ref.at[t], y_buf, y_sem)
        load.start()
        load.wait()
        for hh in range(irreps_here):

            def tile(n, carry):
                cols = pl.ds(pl.multiple_of(n * tile_r, tile_r), tile_r)
                ladder = None
                for s in range(slabs):
                    left = jnp.concatenate(
                        [
                            y_buf[p, hh, s, :, j * ks : (j + 1) * ks]
                            for p in range(n_pair)
                            for j in range(parts_sb)
                        ],
                        axis=0,
                    )
                    term = jnp.dot(left, amps_ref[hh, s, :, cols], preferred_element_type=jnp.float32)
                    ladder = term if ladder is None else ladder + term
                base = rows_ref[dest * cuts + t % cuts, :, hh : hh + 1]
                live = rows_ref[dest * cuts + t % cuts, :, irreps_here + hh : irreps_here + hh + 1]
                occ = occ_ref[hh : hh + 1, cols]
                live_r = occ_ref[irreps_here + hh : irreps_here + hh + 1, cols]
                denom = base - occ
                ratio = jnp.where(live * live_r > 0.5, ladder / denom, 0.0)
                terms[hh : hh + 1, cols] += jnp.sum(ratio * ladder, axis=0, keepdims=True)
                update = jnp.dot(
                    sort_out_ref[...], ratio.astype(jnp.bfloat16), preferred_element_type=jnp.float32
                ).astype(jnp.bfloat16)
                out_buf[t, hh, :, :, cols] = update.reshape(a_chunk, sb_here, tile_r)
                return carry

            lax.fori_loop(0, nrows // tile_r, tile, 0)
        out_copy(t).start()

    terms[...] = jnp.zeros_like(terms)
    for t in range(depth):
        prepare(t)
    for t in range(steps):
        for d in range(1, n_pair):
            pair_copy(t, d).wait_recv()
        own_copy(t).wait()
        compute(t)
        for d in range(1, n_pair):
            pair_copy(t, d).wait_send()
        if t + depth < steps:
            prepare(t + depth)
    for d in range(1, n_virt):
        part_copy(d).start()
    for d in range(1, n_virt):
        part_copy(d).wait()
    mine = terms[:, pl.ds(pl.multiple_of(me_v * e_cols, e_cols), e_cols)]
    for d in range(1, n_virt):
        mine = mine + parts[d - 1]
    energy_ref[...] = mine / energy_scale
    for t in range(steps):
        out_copy(t).wait()


def fused_shards(amplitudes, integrals, virt_counts, pair_counts, pair_list, eps_occ, eps_virt):
    irreps_here, rows, slabs, ks = amplitudes.shape
    n_virt = lax.axis_size("virt")
    n_pair = lax.axis_size("pair")
    nv = integrals.shape[1]
    irreps = integrals.shape[2]
    loc = integrals.shape[3]
    cuts = nv // n_virt // A_SORT
    depth = 4
    a_chunk = A_SORT
    steps = n_virt * cuts
    parts_sb = loc // ks
    sb_here = n_pair * parts_sb
    me_v = lax.axis_index("virt")
    irrep_ids = lax.axis_index("pair") * irreps_here + jnp.arange(irreps_here, dtype=jnp.int32)
    slots = jnp.arange(BLK, dtype=jnp.int32)
    live_d = slots[None, :] < pick_counts(irrep_ids, virt_counts)[:, None]
    dmask = jnp.tile(live_d, (1, ks // BLK)).astype(jnp.bfloat16)
    masked = amplitudes * dmask[:, None, None, :]
    amps = jnp.transpose(masked, (0, 2, 3, 1))

    a_index = jnp.arange(nv, dtype=jnp.int32)
    a_irrep = a_index // BLK
    live_virt = (slots[None, :] < virt_counts[:, None]).astype(jnp.float32)
    b_irrep = jnp.bitwise_xor(a_irrep[None, :], irrep_ids[:, None])
    b_onehot = (b_irrep[..., None] == jnp.arange(irreps, dtype=jnp.int32)).astype(jnp.float32)
    eps_here = lax.dynamic_slice_in_dim(eps_virt.reshape(irreps, BLK), me_v * sb_here, sb_here, axis=1)
    live_here = lax.dynamic_slice_in_dim(live_virt, me_v * sb_here, sb_here, axis=1)
    eps_b = jnp.einsum("hag,gs->hsa", b_onehot, eps_here, precision=lax.Precision.HIGHEST)
    live_b = jnp.einsum("hag,gs->hsa", b_onehot, live_here, precision=lax.Precision.HIGHEST)
    base = eps_virt[None, None, :] + eps_b
    live = live_virt.reshape(-1)[None, None, :] * live_b
    cols = jnp.concatenate([base, live], axis=0)
    cols = cols.reshape(2 * irreps_here, sb_here, steps, a_chunk)
    cols = jnp.transpose(cols, (2, 1, 3, 0)).reshape(steps, sb_here * a_chunk, 2 * irreps_here)

    occ_onehot = pair_list[..., None] == jnp.arange(eps_occ.shape[0], dtype=jnp.int32)
    occ_terms = jnp.sum(jnp.where(occ_onehot, eps_occ, 0.0), axis=-1)
    occ = occ_terms[:, :, 0] + occ_terms[:, :, 1]
    live_rows = jnp.arange(rows, dtype=jnp.int32)[None, :] < pick_counts(irrep_ids, pair_counts)[:, None]
    occ_live = jnp.concatenate([occ, live_rows.astype(jnp.float32)], axis=0)

    a_sort = A_SORT
    n_in = a_sort * irreps
    i_in = jnp.arange(n_in, dtype=jnp.int32)
    from_in = (i_in % a_sort) * irreps + i_in // a_sort
    sort_in = (from_in[:, None] == i_in[None, :]).astype(jnp.bfloat16)
    i_out = jnp.arange(a_chunk * sb_here, dtype=jnp.int32)
    from_out = (i_out % sb_here) * a_chunk + i_out // sb_here
    sort_out = (from_out[:, None] == i_out[None, :]).astype(jnp.bfloat16)

    eri = integrals.reshape(slabs, nv * irreps, loc)
    vmem = pl.BlockSpec(memory_space=pltpu.VMEM)
    hbm = pl.BlockSpec(memory_space=pl.ANY)
    got, _, energy = pl.pallas_call(
        functools.partial(ladder_kernel, n_virt, n_pair, irreps_here, a_chunk, cuts, depth, parts_sb, nv * BLK),
        out_shape=(
            jax.ShapeDtypeStruct((irreps_here, a_chunk * cuts, n_virt, sb_here, rows), jnp.bfloat16),
            jax.ShapeDtypeStruct((steps, n_pair, irreps_here, slabs, a_chunk, loc), jnp.bfloat16),
            jax.ShapeDtypeStruct((irreps_here, rows // n_virt), jnp.float32),
        ),
        in_specs=[hbm, vmem, vmem, vmem, vmem, vmem],
        out_specs=(hbm, hbm, vmem),
        scratch_shapes=[
            pltpu.VMEM((slabs, a_chunk * irreps, loc), jnp.bfloat16),
            pltpu.VMEM((depth, n_pair, irreps_here, slabs, a_chunk, loc), jnp.bfloat16),
            pltpu.VMEM((n_pair, irreps_here, slabs, a_chunk, loc), jnp.bfloat16),
            pltpu.VMEM((steps, irreps_here, a_chunk, sb_here, rows), jnp.bfloat16),
            pltpu.VMEM((irreps_here, rows), jnp.float32),
            pltpu.VMEM((n_virt - 1, irreps_here, rows // n_virt), jnp.float32),
            pltpu.SemaphoreType.DMA,
            pltpu.SemaphoreType.DMA,
            pltpu.SemaphoreType.DMA((depth,)),
            pltpu.SemaphoreType.DMA((cuts,)),
            pltpu.SemaphoreType.DMA((depth, n_pair - 1)),
            pltpu.SemaphoreType.DMA((steps, n_pair - 1)),
            pltpu.SemaphoreType.DMA((steps,)),
            pltpu.SemaphoreType.DMA((steps,)),
            pltpu.SemaphoreType.DMA((n_virt - 1,)),
            pltpu.SemaphoreType.DMA((n_virt - 1,)),
        ],
        compiler_params=pltpu.CompilerParams(
            collective_id=0, has_side_effects=True, vmem_limit_bytes=60 * 1024 * 1024
        ),
    )(eri, amps, cols, occ_live, sort_in, sort_out)
    flat = got.reshape(irreps_here, a_chunk * cuts * BLK, rows)
    update = jnp.transpose(flat, (0, 2, 1))
    return (update, energy)


def solution(mesh):
    placed = (
        P("pair", None, None, None),
        P(None, None, None, ("virt", "pair")),
        P(),
        P(),
        P("pair", None, None),
        P(),
        P(),
    )

    def run(*arrays):
        amplitudes, integrals = arrays[:2]
        loc = integrals.shape[3] // (mesh.shape["virt"] * mesh.shape["pair"])
        whole_slots = loc % amplitudes.shape[3] == 0
        whole_chunks = (integrals.shape[1] // mesh.shape["virt"]) % A_SORT == 0
        body = fused_shards if whole_slots and whole_chunks else shards
        return jax.shard_map(
            body,
            mesh=mesh,
            in_specs=placed,
            out_specs=(P("pair", None, "virt"), P("pair", "virt")),
            check_vma=False,
        )(*arrays)

    return run
```

```python
import functools

import jax
import jax.numpy as jnp
from jax import lax
from jax.experimental import pallas as pl
from jax.experimental.pallas import tpu as pltpu
from jax.sharding import PartitionSpec as P

IRREPS = 8
NV = 512
BLK = 64
CS = 16
SLABS = 2
A_SORT = 32
MESH = pl.DeviceIdType.MESH


def pick_counts(irrep_ids, table):
    onehot = irrep_ids[..., None] == jnp.arange(table.shape[0], dtype=jnp.int32)
    return jnp.sum(jnp.where(onehot, table, 0), axis=-1)


def shards(amplitudes, integrals, virt_counts, pair_counts, pair_list, eps_occ, eps_virt):
    local_irreps = amplitudes.shape[0]
    rows = amplitudes.shape[1]
    width = amplitudes.shape[3]
    n_virt = lax.axis_size("virt")
    n_pair = lax.axis_size("pair")
    a_local = NV // n_virt
    irrep_ids = lax.axis_index("pair") * local_irreps + jnp.arange(local_irreps, dtype=jnp.int32)
    slots = jnp.arange(BLK, dtype=jnp.int32)
    live_d = slots[None, :] < pick_counts(irrep_ids, virt_counts)[:, None]
    dmask = jnp.tile(live_d, (1, CS)).astype(jnp.bfloat16)
    masked = amplitudes * dmask[:, None, None, :]
    ladder = jnp.zeros((local_irreps, rows, a_local, BLK), jnp.float32)
    for s in range(SLABS):
        piece = integrals[s]
        moved = lax.all_to_all(
            lax.all_to_all(piece, "virt", split_axis=0, concat_axis=2, tiled=True),
            "pair",
            split_axis=1,
            concat_axis=2,
            tiled=True,
        )
        moved = moved.reshape(a_local, local_irreps, n_pair, n_virt, -1)
        moved = jnp.transpose(moved, (0, 1, 3, 2, 4)).reshape(a_local, local_irreps, BLK, width)
        ladder = ladder + jnp.einsum(
            "hrk,ahsk->hras", masked[:, :, s, :], moved, preferred_element_type=jnp.float32
        )
    a_global = lax.axis_index("virt") * a_local + jnp.arange(a_local, dtype=jnp.int32)
    a_irrep = a_global // BLK
    a_slot = a_global % BLK
    live_a = a_slot < pick_counts(a_irrep, virt_counts)
    eps_a = lax.dynamic_slice_in_dim(eps_virt, lax.axis_index("virt") * a_local, a_local)
    b_irrep = jnp.bitwise_xor(a_irrep[None, :], irrep_ids[:, None])
    b_onehot = (b_irrep[..., None] == jnp.arange(IRREPS, dtype=jnp.int32)).astype(jnp.float32)
    eps_table = eps_virt.reshape(IRREPS, BLK)
    eps_b = jnp.einsum("hag,gs->has", b_onehot, eps_table, precision=lax.Precision.HIGHEST)
    live_b = slots[None, None, :] < pick_counts(b_irrep, virt_counts)[..., None]
    occ_onehot = pair_list[..., None] == jnp.arange(eps_occ.shape[0], dtype=jnp.int32)
    occ_terms = jnp.sum(jnp.where(occ_onehot, eps_occ, 0.0), axis=-1)
    occ = occ_terms[:, :, 0] + occ_terms[:, :, 1]
    live_rows = (
        jnp.arange(rows, dtype=jnp.int32)[None, :] < pick_counts(irrep_ids, pair_counts)[:, None]
    )
    denom = (eps_a[None, :, None] + eps_b)[:, None, :, :] - occ[:, :, None, None]
    live = live_rows[:, :, None, None] & live_a[None, None, :, None] & live_b[:, None, :, :]
    ratio = jnp.where(live, ladder / denom, jnp.zeros_like(ladder))
    update = ratio.astype(jnp.bfloat16).reshape(local_irreps, rows, a_local * BLK)
    partial_value = jnp.sum(ratio * ladder, axis=(2, 3)) / (NV * BLK)
    energy = lax.psum_scatter(partial_value, "virt", scatter_dimension=1, tiled=True)
    return (update, energy)


def flip_bits(index, pattern, count):
    flipped = 0
    weight = 1
    while weight < count:
        bit = (index // weight) % 2
        mine = (pattern // weight) % 2
        flipped = flipped + weight * (bit + mine - 2 * bit * mine)
        weight *= 2
    return flipped


def send_order(count):
    half, quarter = count // 2, count // 4
    far = list(range(count - 1, half - 1, -1))
    near = list(range(half - 1, -1, -1))
    mixed = [d for both in zip(far[:quarter], near[:quarter]) for d in both]
    return mixed + far[quarter:] + near[quarter:]


def ladder_kernel(
    n_virt, n_pair, irreps_here, a_chunk, cuts, depth, parts_sb, energy_scale,
    eri_ref, amps_ref, dmask_ref, rows_ref, occ_ref, sort_in_ref, sort_out_ref,
    got_ref, recv_ref, energy_ref,
    x_buf, stage, y_buf, out_buf, terms, parts,
    x_sem, y_sem, own_sem, keep_sem, send_sem, recv_sem, out_sem, got_sem, term_sem, part_sem,
):
    me_v = lax.axis_index("virt")
    me_p = lax.axis_index("pair")
    slabs = eri_ref.shape[0]
    loc = eri_ref.shape[2]
    irreps = irreps_here * n_pair
    ks = amps_ref.shape[2]
    nrows = amps_ref.shape[3]
    sort_rows = sort_in_ref.shape[0]
    a_sort = sort_rows // irreps
    sb_here = n_pair * parts_sb
    chunk_rows = a_chunk * irreps
    steps = n_virt * cuts
    order = send_order(n_virt)
    e_cols = nrows // n_virt
    tile_n = 512
    tile_r = 256

    barrier = pltpu.get_barrier_semaphore()
    for d in range(1, n_pair):
        pl.semaphore_signal(barrier, inc=1, device_id=(me_v, flip_bits(me_p, d, n_pair)), device_id_type=MESH)
    for d in range(1, n_virt):
        pl.semaphore_signal(barrier, inc=1, device_id=(flip_bits(me_v, d, n_virt), me_p), device_id_type=MESH)
    pl.semaphore_wait(barrier, n_pair - 1 + n_virt - 1)

    def target(t):
        return flip_bits(me_v, order[t // cuts], n_virt)

    def pair_copy(t, d):
        peer = flip_bits(me_p, d, n_pair)
        return pltpu.make_async_remote_copy(
            src_ref=stage.at[t % depth, peer],
            dst_ref=recv_ref.at[t, me_p],
            send_sem=send_sem.at[t % depth, d - 1],
            recv_sem=recv_sem.at[t, d - 1],
            device_id=(me_v, peer),
            device_id_type=MESH,
        )

    def own_copy(t):
        return pltpu.make_async_copy(stage.at[t % depth, me_p], recv_ref.at[t, me_p], own_sem.at[t % depth])

    def out_copy(t):
        dest = target(t)
        cut = t % cuts
        there = got_ref.at[:, cut * a_chunk : (cut + 1) * a_chunk, me_v]
        if order[t // cuts] == 0:
            return pltpu.make_async_copy(out_buf.at[t], there, keep_sem.at[cut])
        return pltpu.make_async_remote_copy(
            src_ref=out_buf.at[t],
            dst_ref=there,
            send_sem=out_sem.at[t],
            recv_sem=got_sem.at[t],
            device_id=(dest, me_p),
            device_id_type=MESH,
        )

    def part_copy(d):
        dest = flip_bits(me_v, d, n_virt)
        cols = pl.ds(pl.multiple_of(dest * e_cols, e_cols), e_cols)
        return pltpu.make_async_remote_copy(
            src_ref=terms.at[:, cols],
            dst_ref=parts.at[d - 1],
            send_sem=term_sem.at[d - 1],
            recv_sem=part_sem.at[d - 1],
            device_id=(dest, me_p),
            device_id_type=MESH,
        )

    def prepare(t):
        dest = target(t)
        load = pltpu.make_async_copy(
            eri_ref.at[:, pl.ds(pl.multiple_of((dest * cuts + t % cuts) * chunk_rows, chunk_rows), chunk_rows), :], x_buf, x_sem
        )
        load.start()
        load.wait()

        def sort_tile(n, carry):
            cols = pl.ds(pl.multiple_of(n * tile_n, tile_n), tile_n)
            for s in range(slabs):
                for q in range(a_chunk // a_sort):
                    block = x_buf[s, q * sort_rows : (q + 1) * sort_rows, cols]
                    sorted_rows = jnp.dot(
                        sort_in_ref[...], block, preferred_element_type=jnp.float32
                    ).astype(jnp.bfloat16)
                    for h in range(irreps):
                        stage[
                            t % depth, h // irreps_here, h % irreps_here, s, q * a_sort : (q + 1) * a_sort, cols
                        ] = sorted_rows[h * a_sort : (h + 1) * a_sort]
            return carry

        lax.fori_loop(0, loc // tile_n, sort_tile, 0)
        for d in range(1, n_pair):
            pair_copy(t, d).start()
        own_copy(t).start()

    def compute(t):
        dest = target(t)
        load = pltpu.make_async_copy(recv_ref.at[t], y_buf, y_sem)
        load.start()
        load.wait()
        for hh in range(irreps_here):

            def tile(n, carry):
                cols = pl.ds(pl.multiple_of(n * tile_r, tile_r), tile_r)
                ladder = None
                for s in range(slabs):
                    left = jnp.concatenate(
                        [
                            y_buf[p, hh, s, :, j * ks : (j + 1) * ks]
                            for p in range(n_pair)
                            for j in range(parts_sb)
                        ],
                        axis=0,
                    )
                    left = left * dmask_ref[hh : hh + 1, :]
                    term = jnp.dot(left, amps_ref[hh, s, :, cols], preferred_element_type=jnp.float32)
                    ladder = term if ladder is None else ladder + term
                base = rows_ref[dest * cuts + t % cuts, :, hh : hh + 1]
                live = rows_ref[dest * cuts + t % cuts, :, irreps_here + hh : irreps_here + hh + 1]
                occ = occ_ref[hh : hh + 1, cols]
                live_r = occ_ref[irreps_here + hh : irreps_here + hh + 1, cols]
                denom = base - occ
                ratio = jnp.where(live * live_r > 0.5, ladder / denom, 0.0)
                terms[hh : hh + 1, cols] += jnp.sum(ratio * ladder, axis=0, keepdims=True)
                update = jnp.dot(
                    sort_out_ref[...], ratio.astype(jnp.bfloat16), preferred_element_type=jnp.float32
                ).astype(jnp.bfloat16)
                out_buf[t, hh, :, :, cols] = update.reshape(a_chunk, sb_here, tile_r)
                return carry

            lax.fori_loop(0, nrows // tile_r, tile, 0)
        out_copy(t).start()

    terms[...] = jnp.zeros_like(terms)
    for t in range(depth):
        prepare(t)
    for t in range(steps):
        for d in range(1, n_pair):
            pair_copy(t, d).wait_recv()
        own_copy(t).wait()
        compute(t)
        for d in range(1, n_pair):
            pair_copy(t, d).wait_send()
        if t + depth < steps:
            prepare(t + depth)
    for d in range(1, n_virt):
        part_copy(d).start()
    for d in range(1, n_virt):
        part_copy(d).wait()
    mine = terms[:, pl.ds(pl.multiple_of(me_v * e_cols, e_cols), e_cols)]
    for d in range(1, n_virt):
        mine = mine + parts[d - 1]
    energy_ref[...] = mine / energy_scale
    for t in range(steps):
        out_copy(t).wait()


def fused_shards(amplitudes, integrals, virt_counts, pair_counts, pair_list, eps_occ, eps_virt):
    irreps_here, rows, slabs, ks = amplitudes.shape
    n_virt = lax.axis_size("virt")
    n_pair = lax.axis_size("pair")
    nv = integrals.shape[1]
    irreps = integrals.shape[2]
    loc = integrals.shape[3]
    cuts = nv // n_virt // A_SORT
    depth = 4
    a_chunk = A_SORT
    steps = n_virt * cuts
    parts_sb = loc // ks
    sb_here = n_pair * parts_sb
    me_v = lax.axis_index("virt")
    irrep_ids = lax.axis_index("pair") * irreps_here + jnp.arange(irreps_here, dtype=jnp.int32)
    slots = jnp.arange(BLK, dtype=jnp.int32)
    live_d = slots[None, :] < pick_counts(irrep_ids, virt_counts)[:, None]
    dmask = jnp.tile(live_d, (1, ks // BLK)).astype(jnp.bfloat16)
    amps = jnp.transpose(amplitudes, (0, 2, 3, 1))

    a_index = jnp.arange(nv, dtype=jnp.int32)
    a_irrep = a_index // BLK
    live_virt = (slots[None, :] < virt_counts[:, None]).astype(jnp.float32)
    b_irrep = jnp.bitwise_xor(a_irrep[None, :], irrep_ids[:, None])
    b_onehot = (b_irrep[..., None] == jnp.arange(irreps, dtype=jnp.int32)).astype(jnp.float32)
    eps_here = lax.dynamic_slice_in_dim(eps_virt.reshape(irreps, BLK), me_v * sb_here, sb_here, axis=1)
    live_here = lax.dynamic_slice_in_dim(live_virt, me_v * sb_here, sb_here, axis=1)
    eps_b = jnp.einsum("hag,gs->hsa", b_onehot, eps_here, precision=lax.Precision.HIGHEST)
    live_b = jnp.einsum("hag,gs->hsa", b_onehot, live_here, precision=lax.Precision.HIGHEST)
    base = eps_virt[None, None, :] + eps_b
    live = live_virt.reshape(-1)[None, None, :] * live_b
    cols = jnp.concatenate([base, live], axis=0)
    cols = cols.reshape(2 * irreps_here, sb_here, steps, a_chunk)
    cols = jnp.transpose(cols, (2, 1, 3, 0)).reshape(steps, sb_here * a_chunk, 2 * irreps_here)

    occ_onehot = pair_list[..., None] == jnp.arange(eps_occ.shape[0], dtype=jnp.int32)
    occ_terms = jnp.sum(jnp.where(occ_onehot, eps_occ, 0.0), axis=-1)
    occ = occ_terms[:, :, 0] + occ_terms[:, :, 1]
    live_rows = jnp.arange(rows, dtype=jnp.int32)[None, :] < pick_counts(irrep_ids, pair_counts)[:, None]
    occ_live = jnp.concatenate([occ, live_rows.astype(jnp.float32)], axis=0)

    a_sort = A_SORT
    n_in = a_sort * irreps
    i_in = jnp.arange(n_in, dtype=jnp.int32)
    from_in = (i_in % a_sort) * irreps + i_in // a_sort
    sort_in = (from_in[:, None] == i_in[None, :]).astype(jnp.bfloat16)
    i_out = jnp.arange(a_chunk * sb_here, dtype=jnp.int32)
    from_out = (i_out % sb_here) * a_chunk + i_out // sb_here
    sort_out = (from_out[:, None] == i_out[None, :]).astype(jnp.bfloat16)

    eri = integrals.reshape(slabs, nv * irreps, loc)
    vmem = pl.BlockSpec(memory_space=pltpu.VMEM)
    hbm = pl.BlockSpec(memory_space=pl.ANY)
    got, _, energy = pl.pallas_call(
        functools.partial(ladder_kernel, n_virt, n_pair, irreps_here, a_chunk, cuts, depth, parts_sb, nv * BLK),
        out_shape=(
            jax.ShapeDtypeStruct((irreps_here, a_chunk * cuts, n_virt, sb_here, rows), jnp.bfloat16),
            jax.ShapeDtypeStruct((steps, n_pair, irreps_here, slabs, a_chunk, loc), jnp.bfloat16),
            jax.ShapeDtypeStruct((irreps_here, rows // n_virt), jnp.float32),
        ),
        in_specs=[hbm, vmem, vmem, vmem, vmem, vmem, vmem],
        out_specs=(hbm, hbm, vmem),
        scratch_shapes=[
            pltpu.VMEM((slabs, a_chunk * irreps, loc), jnp.bfloat16),
            pltpu.VMEM((depth, n_pair, irreps_here, slabs, a_chunk, loc), jnp.bfloat16),
            pltpu.VMEM((n_pair, irreps_here, slabs, a_chunk, loc), jnp.bfloat16),
            pltpu.VMEM((steps, irreps_here, a_chunk, sb_here, rows), jnp.bfloat16),
            pltpu.VMEM((irreps_here, rows), jnp.float32),
            pltpu.VMEM((n_virt - 1, irreps_here, rows // n_virt), jnp.float32),
            pltpu.SemaphoreType.DMA,
            pltpu.SemaphoreType.DMA,
            pltpu.SemaphoreType.DMA((depth,)),
            pltpu.SemaphoreType.DMA((cuts,)),
            pltpu.SemaphoreType.DMA((depth, n_pair - 1)),
            pltpu.SemaphoreType.DMA((steps, n_pair - 1)),
            pltpu.SemaphoreType.DMA((steps,)),
            pltpu.SemaphoreType.DMA((steps,)),
            pltpu.SemaphoreType.DMA((n_virt - 1,)),
            pltpu.SemaphoreType.DMA((n_virt - 1,)),
        ],
        compiler_params=pltpu.CompilerParams(
            collective_id=0, has_side_effects=True, vmem_limit_bytes=60 * 1024 * 1024
        ),
    )(eri, amps, dmask, cols, occ_live, sort_in, sort_out)
    flat = got.reshape(irreps_here, a_chunk * cuts * BLK, rows)
    update = jnp.transpose(flat, (0, 2, 1))
    return (update, energy)


def solution(mesh):
    placed = (
        P("pair", None, None, None),
        P(None, None, None, ("virt", "pair")),
        P(),
        P(),
        P("pair", None, None),
        P(),
        P(),
    )

    def run(*arrays):
        amplitudes, integrals = arrays[:2]
        loc = integrals.shape[3] // (mesh.shape["virt"] * mesh.shape["pair"])
        whole_slots = loc % amplitudes.shape[3] == 0
        whole_chunks = (integrals.shape[1] // mesh.shape["virt"]) % A_SORT == 0
        body = fused_shards if whole_slots and whole_chunks else shards
        return jax.shard_map(
            body,
            mesh=mesh,
            in_specs=placed,
            out_specs=(P("pair", None, "virt"), P("pair", "virt")),
            check_vma=False,
        )(*arrays)

    return run
```
